512 devices in a mesh: row: 16 (over y, z_lo), col: 32 (over z_hi, x, core).
Axes of the slice: x: 4, y: 8, z: 8 (z_hi: 4, z_lo: 2; z = z_hi * 2 + z_lo), core: 2. Of those that a mesh axis runs over, the one named last changes fastest.
Arguments:
- amplitudes: bfloat16 [16384, 16384], P('row', 'col'), may hold values from -6 to 6
- df_factors: bfloat16 [16384, 1024], P('col', 'row'), may hold values from -0.375 to 0.375
- ladder: bfloat16 [1024, 1024], P(('row', 'col')), may hold values from -0.1875 to 0.1875
- occ_energy: float32 [200], replicated, may hold values from -2.5 to -0.3
- occ_index: int32 [32], replicated, may hold values from 0 to 199
- vir_energy: float32 [512], replicated, may hold values from 0.3 to 3
- vir_map: int32 [512], replicated, may hold values from 0 to 511, each once
Outputs:
- residual_update: bfloat16 [16384, 16384], P('row', 'col')
The draws below stay inside these ranges and needn't reach their ends.
All inputs are finite; a program needn't handle non-finite values.
Results may differ from the reference program's by a relative error of at most 0.0045.
The reference program's roundings to bfloat16 on the way (of `combined`, `fitted` and `hole_term`) count: a program that leaves them out, or rounds other values in their place, can miss the bound.
Values may be sent and summed in bfloat16 or wider, within the bound.
No kernel may reach another device: no remote copies, remote signals or barrier semaphores. Data moves between devices by JAX's collectives and lax.ppermute only.
A program may use at most 64 MiB of HBM per device.

```python
import jax
import jax.numpy as jnp
from jax import lax

VIR = 512
AUX = 1024
NOCC = 200
OCC = 32
ORDER = 16384
PAIRS = 1024


def with_ends(drawn, own_key, low, high):
    spot = [jax.random.randint(jax.random.fold_in(own_key, axis), (), 0, length) for axis, length in enumerate(drawn.shape)]
    longest = drawn.shape.index(max(drawn.shape))
    beside = spot[:longest] + [(spot[longest] + 1) % drawn.shape[longest]] + spot[longest + 1:]
    return drawn.at[tuple(spot)].set(low).at[tuple(beside)].set(high)


def with_spikes(drawn, rng, source, target, shards_of, factor):
    owner, partner = [(jnp.arange(drawn.shape[position]) // (drawn.shape[position] // shards_of)).reshape([-1 if axis == position else 1 for axis in range(drawn.ndim)]) for position in (source, target)]
    chosen = jax.random.permutation(rng, shards_of)[partner]
    strong = (owner == chosen) | (owner == (partner + shards_of // 2) % shards_of)
    return jnp.where(strong, factor * drawn, drawn)


def steps_of(own_key, extent, split, smallest, high):
    loudness = 1.0
    for position, parts in split:
        heights = jax.random.uniform(jax.random.fold_in(jax.random.fold_in(own_key, 6), position), (parts,), jnp.float32, smallest / len(split), high / len(split))
        loudness = loudness * jnp.repeat(jnp.exp(heights), extent[position] // parts).reshape((-1,) + (1,) * (len(extent) - 1 - position))
    return loudness


def gaussian(rng, dims, width, limit, shards=(), held_as=jnp.bfloat16):
    entries = width * jax.random.normal(rng, dims, jnp.float32)
    if shards:
        entries = entries * steps_of(rng, dims, shards, -0.22, 0.18)
    return jnp.clip(entries, -limit, limit).astype(held_as)


def heavy_noise(stream_key, extent, width, bound, shards, heavy, kind=jnp.bfloat16):
    drawn = width * jax.random.normal(stream_key, extent, jnp.float32)
    if shards:
        drawn = drawn * steps_of(stream_key, extent, shards, -0.22, 0.18)
    return jnp.clip(with_spikes(drawn, jax.random.fold_in(stream_key, 3), *heavy), -bound, bound).astype(kind)


def setup_inputs(seed: int = 0) -> dict:
    key_of = jax.random.split(jax.random.key(seed), 8)
    return {
        "amplitudes": gaussian(key_of[0], (ORDER, ORDER), 1.0, 6.0, ((0, 16), (1, 32))),
        "df_factors": heavy_noise(key_of[1], (ORDER, AUX), AUX ** -0.5, 0.375, ((0, 32), (1, 16)), (0, 1, 32, 2.75)),
        "ladder": gaussian(key_of[2], (PAIRS, PAIRS), PAIRS ** -0.5, 0.1875, ((0, 512),)),
        "occ_energy": jnp.clip(jax.random.uniform(key_of[3], (NOCC,), jnp.float32, -2.5, -0.3), -2.5, -0.3),
        "occ_index": with_ends(jax.random.randint(key_of[4], (OCC,), 0, NOCC), jax.random.fold_in(key_of[4], 1), 0, NOCC - 1).astype(jnp.int32),
        "vir_energy": jnp.clip(jax.random.uniform(key_of[5], (VIR,), jnp.float32, 0.3, 3.0), 0.3, 3.0),
        "vir_map": jax.random.permutation(key_of[6], VIR).astype(jnp.int32),
    }


def reference(amplitudes, df_factors, ladder, occ_energy, occ_index, vir_energy, vir_map):
    order = OCC * VIR
    blocks = amplitudes.reshape(OCC, VIR, OCC, VIR)
    factors_wide = df_factors.astype(jnp.float32)

    def fit_rows(occ):
        slab = lax.dynamic_index_in_dim(blocks, occ, 0, keepdims=False)
        mirror = jnp.transpose(slab, (2, 1, 0))
        combined = (2.0 * slab.astype(jnp.float32) - mirror.astype(jnp.float32)).astype(jnp.bfloat16)
        return jnp.dot(combined.reshape(VIR, order).astype(jnp.float32), factors_wide)

    fitted = lax.map(fit_rows, jnp.arange(OCC, dtype=jnp.int32)).reshape(order, AUX).astype(jnp.bfloat16)
    pair_major = jnp.transpose(blocks, (0, 2, 1, 3)).reshape(OCC * OCC, VIR * VIR).astype(jnp.float32)
    ladder_rows = ladder.reshape(OCC, OCC, OCC * OCC).astype(jnp.float32)
    row_energy = occ_energy[occ_index]
    virtual = vir_energy[vir_map]

    def residual_rows(occ):
        fit_block = lax.dynamic_slice_in_dim(fitted, occ * VIR, VIR, 0).astype(jnp.float32)
        coulomb = jnp.dot(fit_block, factors_wide.T).reshape(VIR, OCC, VIR)
        weights = lax.dynamic_index_in_dim(ladder_rows, occ, 0, keepdims=False)
        hole_term = jnp.dot(weights, pair_major).astype(jnp.bfloat16)
        hole_term = lax.optimization_barrier(hole_term).astype(jnp.float32)
        hole_term = jnp.transpose(hole_term.reshape(OCC, VIR, VIR), (1, 0, 2))
        own_energy = lax.dynamic_index_in_dim(row_energy, occ, 0, keepdims=False)
        denominator = own_energy + row_energy[None, :, None] - virtual[:, None, None] - virtual[None, None, :]
        return ((coulomb + hole_term) / denominator).astype(jnp.bfloat16)

    result = lax.map(residual_rows, jnp.arange(OCC, dtype=jnp.int32))
    return result.reshape(order, order)
```

```python
import jax
import jax.numpy as jnp
from jax import lax
from jax.sharding import Mesh, PartitionSpec as P

VIR = 512
BF = jnp.bfloat16
F32 = jnp.float32
CHIPS = ("y", "zl", "zh", "x")


def exchange(value, axes):
    return lax.all_to_all(value, axes, split_axis=0, concat_axis=0, tiled=True)


def spread(value, axes):
    count = lax.axis_size(axes)
    return exchange(jnp.broadcast_to(value[None], (count, *value.shape)), axes)


def partner(value):
    return lax.ppermute(value, "core", [(0, 1), (1, 0)])


def lookup(values, positions):
    table = jnp.arange(values.shape[0], dtype=jnp.int32)
    matches = positions[:, None] == table[None, :]
    return jnp.sum(jnp.where(matches, values[None, :], 0.0), axis=1)


def dot(a, b, ca, cb):
    return lax.dot_general(a, b, (((ca,), (cb,)), ((), ())), preferred_element_type=F32)


def shards(amplitudes, df_factors, ladder, occ_energy, occ_index, vir_energy, vir_map):
    core = lax.axis_index("core")
    blocks = amplitudes.reshape(2, VIR, VIR)
    mirror = jnp.transpose(blocks, (0, 2, 1))
    combined = (2.0 * blocks.astype(F32) - mirror.astype(F32)).astype(BF).reshape(1024, 512)
    combined_other = partner(combined)

    tall = jnp.transpose(df_factors)
    halves = jnp.broadcast_to(tall.reshape(1, 2, 32, 512), (16, 2, 32, 512)).reshape(32, 32, 512)
    factors = exchange(halves, ("y", "zl", "core")).reshape(16, 2, 32, 512)
    own = lax.dynamic_index_in_dim(factors, core, 1, keepdims=False).reshape(512, 512)
    other = lax.dynamic_index_in_dim(factors, 1 - core, 1, keepdims=False).reshape(512, 512)
    partial = (dot(combined, own, 1, 1) + dot(combined_other, other, 1, 1)).astype(BF)
    pieces = exchange(partial.reshape(16, 64, 512), ("zh", "x"))
    shared = jnp.sum(pieces.astype(F32), axis=0).astype(BF)
    fitted = spread(shared, ("zh",))
    fitted = spread(fitted, ("x",))
    fitted = jnp.transpose(fitted, (1, 0, 2, 3)).reshape(1024, 512)
    fitted_other = partner(fitted)
    other_back = partner(other)
    coulomb = dot(fitted, own, 1, 0) + dot(fitted_other, other_back, 1, 0)

    tiles = amplitudes.reshape(2, 64, 8, 4, 128).transpose(1, 3, 0, 2, 4).reshape(256, 2, 8, 128)
    pairs = exchange(tiles, CHIPS).reshape(512, 1024)
    pairs_other = partner(pairs)
    rows = ladder.reshape(2, 16, 2, 16, 2).transpose(0, 4, 1, 3, 2).reshape(2, 2, 512)
    mine = spread(rows, ("y", "zl", "zh")).reshape(64, 2, 2, 512)
    mine = exchange(jnp.broadcast_to(mine.transpose(1, 0, 2, 3)[None], (4, 2, 64, 2, 512)).reshape(8, 64, 2, 512), ("x", "core"))
    mine = mine.reshape(4, 2, 16, 2, 2, 2, 512).transpose(5, 2, 4, 0, 1, 3, 6).reshape(2, 512, 512)
    weight_own = lax.dynamic_index_in_dim(mine, core, 0, keepdims=False)
    weight_other = lax.dynamic_index_in_dim(mine, 1 - core, 0, keepdims=False)
    hole = (dot(weight_own, pairs, 1, 0) + dot(weight_other, pairs_other, 1, 0)).astype(BF)
    hole = exchange(hole.reshape(256, 2, 8, 128), CHIPS)
    hole = hole.reshape(64, 4, 2, 8, 128).transpose(2, 0, 3, 1, 4).reshape(2, VIR, VIR)

    row = lax.axis_index(("y", "zl"))
    col = lax.axis_index(("zh", "x", "core"))
    row_energy = lookup(occ_energy, lax.dynamic_slice_in_dim(occ_index, row * 2, 2))
    col_energy = lookup(occ_energy, lax.dynamic_slice_in_dim(occ_index, col, 1))
    virtual = lookup(vir_energy, vir_map)
    denominator = row_energy[:, None, None] + col_energy[0] - virtual[None, :, None] - virtual[None, None, :]
    summed = coulomb.reshape(2, VIR, VIR) + hole.astype(F32)
    return (summed / denominator).astype(BF).reshape(1024, 512)


def solution(mesh):
    fine = Mesh(mesh.devices.reshape(8, 2, 4, 4, 2), ("y", "zl", "zh", "x", "core"))
    row, col = ("y", "zl"), ("zh", "x", "core")
    placed = (P(row, col), P(col, row), P(row + col, None), P(), P(), P(), P())
    return jax.shard_map(shards, mesh=fine, in_specs=placed, out_specs=P(row, col), check_vma=False)
```

```python
import jax
import jax.numpy as jnp
from jax import lax
from jax.sharding import Mesh, PartitionSpec as P

VIR = 512
BF = jnp.bfloat16
F32 = jnp.float32
CHIPS = ("y", "zl", "zh", "x")


def exchange(value, axes):
    return lax.all_to_all(value, axes, split_axis=0, concat_axis=0, tiled=True)


def shifted(value, axis, step):
    count = lax.axis_size(axis)
    return lax.ppermute(value, axis, [(i, (i + step) % count) for i in range(count)])


def partner(value):
    return shifted(value, "core", 1)


def gather_ring(value, axis):
    count = lax.axis_size(axis)
    me = lax.axis_index(axis)
    everyone = jnp.zeros((count, *value.shape), value.dtype)
    for step in range(count):
        near = shifted(value, axis, step) if step else value
        everyone = lax.dynamic_update_index_in_dim(everyone, near, (me - step) % count, 0)
    return everyone


def pieces_ring(value, axis):
    count = lax.axis_size(axis)
    me = lax.axis_index(axis)
    pieces = []
    for step in range(count):
        piece = lax.dynamic_index_in_dim(value, (me + step) % count, 0, keepdims=False)
        pieces.append(shifted(piece, axis, step) if step else piece)
    return pieces


def spread(value, axes):
    count = lax.axis_size(axes)
    return exchange(jnp.broadcast_to(value[None], (count, *value.shape)), axes)


def lookup(values, positions):
    table = jnp.arange(values.shape[0], dtype=jnp.int32)
    matches = positions[:, None] == table[None, :]
    return jnp.sum(jnp.where(matches, values[None, :], 0.0), axis=1)


def dot(a, b, ca, cb):
    return lax.dot_general(a, b, (((ca,), (cb,)), ((), ())), preferred_element_type=F32)


def shards(amplitudes, df_factors, ladder, occ_energy, occ_index, vir_energy, vir_map):
    core = lax.axis_index("core")
    blocks = amplitudes.reshape(2, VIR, VIR)

    tall = jnp.transpose(df_factors).reshape(2, 4, 8, 4, 128).transpose(0, 1, 3, 2, 4).reshape(2, 16, 8, 128)
    place = jnp.arange(1024, dtype=jnp.int32)
    source = (place // 32 % 16) * 64 + (place % 2) * 32 + (place // 2 % 16) * 2 + place // 512
    chosen = (jnp.arange(1024, dtype=jnp.int32)[:, None] == source[None, :]).astype(BF)
    rows = dot(ladder, chosen, 1, 0).astype(BF)
    swapped = jnp.concatenate([rows[1:, 512:], rows[1:, :512]], axis=1)
    rows = jnp.concatenate([rows[:1], swapped]).reshape(2, 1, 8, 128)
    send = jnp.concatenate([tall, rows], axis=1)
    send = jnp.broadcast_to(send[None], (16, 2, 17, 8, 128)).reshape(32, 17, 8, 128)
    arrived = exchange(send, ("y", "zl", "core"))
    factors = arrived[:, :16].reshape(16, 2, 4, 4, 8, 128).transpose(0, 1, 2, 4, 3, 5).reshape(16, 2, 32, 512)
    own = lax.dynamic_index_in_dim(factors, core, 1, keepdims=False).reshape(512, 512)
    other = lax.dynamic_index_in_dim(factors, 1 - core, 1, keepdims=False).reshape(512, 512)

    tiles = amplitudes.reshape(2, 64, 8, 4, 128).transpose(1, 3, 0, 2, 4).reshape(256, 2, 8, 128)
    pairs = exchange(tiles, CHIPS)
    weights = gather_ring(arrived[:, 16].reshape(32, 1024), "zh")
    weights = gather_ring(weights, "x")
    weights = weights.reshape(512, 1024)

    mirror = jnp.transpose(blocks, (0, 2, 1))
    combined = (2.0 * blocks.astype(F32) - mirror.astype(F32)).astype(BF).reshape(1024, 512)
    combined_other = partner(combined)
    partial = (dot(combined, own, 1, 1) + dot(combined_other, other, 1, 1)).astype(BF)
    pieces = pieces_ring(partial.reshape(4, 256, 512), "x")
    shared = sum(piece.astype(F32) for piece in pieces)
    shared = exchange(shared.reshape(4, 64, 512), ("zh",))
    shared = jnp.sum(shared, axis=0).astype(BF)
    fitted = spread(shared, ("zh",)).reshape(256, 512)
    fitted = gather_ring(fitted, "x").reshape(1024, 512)
    fitted_other = partner(fitted)
    other_back = partner(other)
    coulomb = dot(fitted, own, 1, 0) + dot(fitted_other, other_back, 1, 0)

    pairs = pairs.reshape(512, 1024)
    pairs_other = partner(pairs)
    hole = (dot(weights[:, :512], pairs, 1, 0) + dot(weights[:, 512:], pairs_other, 1, 0)).astype(BF)
    hole = hole.reshape(4, 2, 2, 16, 2, 8, 128).transpose(3, 2, 0, 4, 1, 5, 6).reshape(256, 2, 8, 128)
    hole = exchange(hole, CHIPS)
    hole = hole.reshape(64, 4, 2, 8, 128).transpose(2, 0, 3, 1, 4).reshape(2, VIR, VIR)

    row = lax.axis_index(("y", "zl"))
    col = lax.axis_index(("zh", "x", "core"))
    row_energy = lookup(occ_energy, lax.dynamic_slice_in_dim(occ_index, row * 2, 2))
    col_energy = lookup(occ_energy, lax.dynamic_slice_in_dim(occ_index, col, 1))
    virtual = lookup(vir_energy, vir_map)
    denominator = row_energy[:, None, None] + col_energy[0] - virtual[None, :, None] - virtual[None, None, :]
    summed = coulomb.reshape(2, VIR, VIR) + hole.astype(F32)
    return (summed / denominator).astype(BF).reshape(1024, 512)


def solution(mesh):
    fine = Mesh(mesh.devices.reshape(8, 2, 4, 4, 2), ("y", "zl", "zh", "x", "core"))
    row, col = ("y", "zl"), ("zh", "x", "core")
    placed = (P(row, col), P(col, row), P(row + col, None), P(), P(), P(), P())

    return jax.shard_map(shards, mesh=fine, in_specs=placed, out_specs=P(row, col), check_vma=False)
```

```python
import jax
import jax.numpy as jnp
from jax import lax
from jax.sharding import Mesh, PartitionSpec as P

VIR = 512
BF = jnp.bfloat16
F32 = jnp.float32
CHIPS = ("y", "zl", "zh", "x")


def exchange(value, axes):
    return lax.all_to_all(value, axes, split_axis=0, concat_axis=0, tiled=True)


def shifted(value, axis, step):
    count = lax.axis_size(axis)
    return lax.ppermute(value, axis, [(i, (i + step) % count) for i in range(count)])


def partner(value):
    return shifted(value, "core", 1)


def gather_ring(value, axis):
    count = lax.axis_size(axis)
    me = lax.axis_index(axis)
    everyone = jnp.zeros((count, *value.shape), value.dtype)
    for step in range(count):
        near = shifted(value, axis, step) if step else value
        everyone = lax.dynamic_update_index_in_dim(everyone, near, (me - step) % count, 0)
    return everyone


def pieces_ring(value, axis):
    count = lax.axis_size(axis)
    me = lax.axis_index(axis)
    pieces = []
    for step in range(count):
        piece = lax.dynamic_index_in_dim(value, (me + step) % count, 0, keepdims=False)
        pieces.append(shifted(piece, axis, step) if step else piece)
    return pieces


def spread(value, axes):
    count = lax.axis_size(axes)
    return exchange(jnp.broadcast_to(value[None], (count, *value.shape)), axes)


def lookup(values, positions):
    table = jnp.arange(values.shape[0], dtype=jnp.int32)
    matches = positions[:, None] == table[None, :]
    return jnp.sum(jnp.where(matches, values[None, :], 0.0), axis=1)


def dot(a, b, ca, cb):
    return lax.dot_general(a, b, (((ca,), (cb,)), ((), ())), preferred_element_type=F32)


def shards(amplitudes, df_factors, ladder, occ_energy, occ_index, vir_energy, vir_map):
    core = lax.axis_index("core")
    blocks = amplitudes.reshape(2, VIR, VIR)

    tall = jnp.transpose(df_factors).reshape(2, 4, 8, 4, 128).transpose(0, 1, 3, 2, 4).reshape(2, 16, 8, 128)
    place = jnp.arange(1024, dtype=jnp.int32)
    source = (place // 32 % 16) * 64 + (place % 2) * 32 + (place // 2 % 16) * 2 + place // 512
    chosen = (jnp.arange(1024, dtype=jnp.int32)[:, None] == source[None, :]).astype(BF)
    rows = dot(ladder, chosen, 1, 0).astype(BF)
    swapped = jnp.concatenate([rows[1:, 512:], rows[1:, :512]], axis=1)
    rows = jnp.concatenate([rows[:1], swapped]).reshape(2, 1, 8, 128)
    send = jnp.concatenate([tall, rows], axis=1)
    send = jnp.broadcast_to(send[None], (8, 2, 17, 8, 128)).reshape(16, 17, 8, 128)
    near = exchange(send, ("y", "core"))
    far = shifted(near, "zl", 1)

    def half_of(arrived, which):
        tiles = lax.dynamic_index_in_dim(arrived.reshape(8, 2, 17, 8, 128), which, 1, keepdims=False)[:, :16]
        return tiles.reshape(8, 4, 4, 8, 128).transpose(0, 1, 3, 2, 4).reshape(256, 512)

    own = jnp.concatenate([half_of(near, core), half_of(far, core)])
    other = jnp.concatenate([half_of(near, 1 - core), half_of(far, 1 - core)])
    tiles = amplitudes.reshape(2, 64, 8, 4, 128).transpose(1, 3, 0, 2, 4).reshape(256, 2, 8, 128)
    pairs = exchange(tiles, CHIPS)
    near_rows = gather_ring(near[:, 16].reshape(16, 1024), "zh")
    far_rows = shifted(near_rows, "zl", 1)
    first = lax.axis_index("zl") == 0
    weights = jnp.stack(
        [jnp.where(first, near_rows, far_rows), jnp.where(first, far_rows, near_rows)], axis=1
    ).reshape(4, 32, 1024)
    weights = gather_ring(weights, "x")
    weights = weights.reshape(512, 1024)

    mirror = jnp.transpose(blocks, (0, 2, 1))
    combined = (2.0 * blocks.astype(F32) - mirror.astype(F32)).astype(BF).reshape(1024, 512)
    combined_other = partner(combined)
    partial = (dot(combined, own, 1, 1) + dot(combined_other, other, 1, 1)).astype(BF)
    pieces = pieces_ring(partial.reshape(4, 256, 512), "x")
    shared = sum(piece.astype(F32) for piece in pieces)
    shared = exchange(shared.reshape(4, 64, 512), ("zh",))
    shared = jnp.sum(shared, axis=0).astype(BF)
    fitted = spread(shared, ("zh",)).reshape(256, 512)
    fitted = gather_ring(fitted, "x").reshape(1024, 512)
    fitted_other = partner(fitted)
    other_back = partner(other)
    coulomb = dot(fitted, own, 1, 0) + dot(fitted_other, other_back, 1, 0)

    pairs = pairs.reshape(512, 1024)
    pairs_other = partner(pairs)
    hole = (dot(weights[:, :512], pairs, 1, 0) + dot(weights[:, 512:], pairs_other, 1, 0)).astype(BF)
    hole = hole.reshape(4, 2, 2, 2, 8, 2, 8, 128).transpose(4, 3, 2, 0, 5, 1, 6, 7).reshape(256, 2, 8, 128)
    hole = exchange(hole, CHIPS)
    hole = hole.reshape(64, 4, 2, 8, 128).transpose(2, 0, 3, 1, 4).reshape(2, VIR, VIR)

    row = lax.axis_index(("y", "zl"))
    col = lax.axis_index(("zh", "x", "core"))
    row_energy = lookup(occ_energy, lax.dynamic_slice_in_dim(occ_index, row * 2, 2))
    col_energy = lookup(occ_energy, lax.dynamic_slice_in_dim(occ_index, col, 1))
    virtual = lookup(vir_energy, vir_map)
    denominator = row_energy[:, None, None] + col_energy[0] - virtual[None, :, None] - virtual[None, None, :]
    summed = coulomb.reshape(2, VIR, VIR) + hole.astype(F32)
    return (summed / denominator).astype(BF).reshape(1024, 512)


def solution(mesh):
    fine = Mesh(mesh.devices.reshape(8, 2, 4, 4, 2), ("y", "zl", "zh", "x", "core"))
    row, col = ("y", "zl"), ("zh", "x", "core")
    placed = (P(row, col), P(col, row), P(row + col, None), P(), P(), P(), P())

    return jax.shard_map(shards, mesh=fine, in_specs=placed, out_specs=P(row, col), check_vma=False)
```

```python
import jax
import jax.numpy as jnp
from jax import lax
from jax.sharding import Mesh, PartitionSpec as P

VIR = 512
BF = jnp.bfloat16
F32 = jnp.float32
CHIPS = ("y", "zl", "zh", "x")


def exchange(value, axes):
    return lax.all_to_all(value, axes, split_axis=0, concat_axis=0, tiled=True)


def shifted(value, axis, step):
    count = lax.axis_size(axis)
    return lax.ppermute(value, axis, [(i, (i + step) % count) for i in range(count)])


def partner(value):
    return shifted(value, "core", 1)


def gather_ring(value, axis):
    count = lax.axis_size(axis)
    me = lax.axis_index(axis)
    everyone = jnp.zeros((count, *value.shape), value.dtype)
    for step in range(count):
        near = shifted(value, axis, step) if step else value
        everyone = lax.dynamic_update_index_in_dim(everyone, near, (me - step) % count, 0)
    return everyone


def pieces_ring(value, axis):
    count = lax.axis_size(axis)
    me = lax.axis_index(axis)
    pieces = []
    for step in range(count):
        piece = lax.dynamic_index_in_dim(value, (me + step) % count, 0, keepdims=False)
        pieces.append(shifted(piece, axis, step) if step else piece)
    return pieces


def spread(value, axes):
    count = lax.axis_size(axes)
    return exchange(jnp.broadcast_to(value[None], (count, *value.shape)), axes)


def lookup(values, positions):
    table = jnp.arange(values.shape[0], dtype=jnp.int32)
    matches = positions[:, None] == table[None, :]
    return jnp.sum(jnp.where(matches, values[None, :], 0.0), axis=1)


def dot(a, b, ca, cb):
    return lax.dot_general(a, b, (((ca,), (cb,)), ((), ())), preferred_element_type=F32)


def shards(amplitudes, df_factors, ladder, occ_energy, occ_index, vir_energy, vir_map):
    core = lax.axis_index("core")
    blocks = amplitudes.reshape(2, VIR, VIR)

    tall = jnp.transpose(df_factors).reshape(2, 4, 8, 4, 128).transpose(0, 1, 3, 2, 4).reshape(2, 16, 8, 128)
    place = jnp.arange(1024, dtype=jnp.int32)
    source = (place // 32 % 16) * 64 + (place % 2) * 32 + (place // 2 % 16) * 2 + place // 512
    chosen = (jnp.arange(1024, dtype=jnp.int32)[:, None] == source[None, :]).astype(BF)
    rows = dot(ladder, chosen, 1, 0).astype(BF)
    swapped = jnp.concatenate([rows[1:, 512:], rows[1:, :512]], axis=1)
    rows = jnp.concatenate([rows[:1], swapped]).reshape(2, 1, 8, 128)
    send = jnp.concatenate([tall, rows], axis=1)
    send = jnp.broadcast_to(send[None], (8, 2, 17, 8, 128)).reshape(16, 17, 8, 128)
    near = exchange(send, ("y", "core"))
    far = shifted(near, "zl", 1)

    def half_of(arrived, which):
        tiles = lax.dynamic_index_in_dim(arrived.reshape(8, 2, 17, 8, 128), which, 1, keepdims=False)[:, :16]
        return tiles.reshape(8, 4, 4, 8, 128).transpose(0, 1, 3, 2, 4).reshape(256, 512)

    own = jnp.concatenate([half_of(near, core), half_of(far, core)])
    other = jnp.concatenate([half_of(near, 1 - core), half_of(far, 1 - core)])
    near_rows = near[:, 16].reshape(8, 1, 2, 1024)
    far_rows = far[:, 16].reshape(8, 1, 2, 1024)
    first = lax.axis_index("zl") == 0
    ladder_rows = jnp.concatenate(
        [jnp.where(first, near_rows, far_rows), jnp.where(first, far_rows, near_rows)], axis=1
    ).reshape(32, 1024)

    tiles = amplitudes.reshape(2, 64, 8, 4, 128).transpose(1, 3, 0, 2, 4).reshape(256, 2, 8, 128)
    pairs = exchange(tiles, CHIPS)
    weights = gather_ring(ladder_rows, "zh")
    weights = gather_ring(weights, "x")
    weights = weights.reshape(512, 1024)

    mirror = jnp.transpose(blocks, (0, 2, 1))
    combined = (2.0 * blocks.astype(F32) - mirror.astype(F32)).astype(BF).reshape(1024, 512)
    combined_other = partner(combined)
    partial = (dot(combined, own, 1, 1) + dot(combined_other, other, 1, 1)).astype(BF)
    pieces = pieces_ring(partial.reshape(4, 256, 512), "x")
    shared = sum(piece.astype(F32) for piece in pieces)
    shared = exchange(shared.reshape(4, 64, 512), ("zh",))
    shared = jnp.sum(shared, axis=0).astype(BF)
    fitted = spread(shared, ("zh",)).reshape(256, 512)
    fitted = gather_ring(fitted, "x").reshape(1024, 512)
    fitted_other = partner(fitted)
    other_back = partner(other)
    coulomb = dot(fitted, own, 1, 0) + dot(fitted_other, other_back, 1, 0)

    pairs = pairs.reshape(512, 1024)
    pairs_other = partner(pairs)
    hole = (dot(weights[:, :512], pairs, 1, 0) + dot(weights[:, 512:], pairs_other, 1, 0)).astype(BF)
    hole = hole.reshape(4, 2, 2, 16, 2, 8, 128).transpose(3, 2, 0, 4, 1, 5, 6).reshape(256, 2, 8, 128)
    hole = exchange(hole, CHIPS)
    hole = hole.reshape(64, 4, 2, 8, 128).transpose(2, 0, 3, 1, 4).reshape(2, VIR, VIR)

    row = lax.axis_index(("y", "zl"))
    col = lax.axis_index(("zh", "x", "core"))
    row_energy = lookup(occ_energy, lax.dynamic_slice_in_dim(occ_index, row * 2, 2))
    col_energy = lookup(occ_energy, lax.dynamic_slice_in_dim(occ_index, col, 1))
    virtual = lookup(vir_energy, vir_map)
    denominator = row_energy[:, None, None] + col_energy[0] - virtual[None, :, None] - virtual[None, None, :]
    summed = coulomb.reshape(2, VIR, VIR) + hole.astype(F32)
    return (summed / denominator).astype(BF).reshape(1024, 512)


def solution(mesh):
    fine = Mesh(mesh.devices.reshape(8, 2, 4, 4, 2), ("y", "zl", "zh", "x", "core"))
    row, col = ("y", "zl"), ("zh", "x", "core")
    placed = (P(row, col), P(col, row), P(row + col, None), P(), P(), P(), P())

    return jax.shard_map(shards, mesh=fine, in_specs=placed, out_specs=P(row, col), check_vma=False)
```
